32 devices in a mesh: freq: 4 (over z), pts: 8 (over y, x, core).
Axes of the slice: x: 2, y: 2, z: 4, core: 2. Of those that a mesh axis runs over, the one named last changes fastest.
Arguments:
- histories: float32 [8, 2048, 4096], P(None, ('freq', 'pts')), may hold values from -6 to 6
- point_weight: float32 [4096], P('pts'), may hold values from 0.5 to 2
- basis: float32 [4096, 4096], P('pts', 'freq'), may hold values from -0.09375 to 0.09375
Outputs:
- coeffs: float32 [8, 2, 256, 4096], P(None, None, 'freq', 'pts')
The draws below stay inside these ranges and needn't reach their ends.
All inputs are finite; a program needn't handle non-finite values.
Results may differ from the reference program's by a relative error of at most 0.00011.
Values sent between devices are 32-bit elements; how exact they have to be, the bound alone decides.
A program may use at most 128 MiB of HBM per device.

```python
import math
import jax
import jax.numpy as jnp
from jax import lax

NT = 2048
F = 256
H = 4096
CASES = 8
P_SIZE = 4096


def level_of(own_key, shape, cuts, least, largest):
    def one(dim, shards_of):
        heights = jax.random.uniform(jax.random.fold_in(jax.random.fold_in(own_key, 6), dim), (shards_of,), jnp.float32, least / len(cuts), largest / len(cuts))
        return jnp.repeat(jnp.exp(heights), shape[dim] // shards_of).reshape((-1,) + (1,) * (len(shape) - dim - 1))

    factor_of = one(*cuts[0])
    for cut in cuts[1:]:
        factor_of = factor_of * one(*cut)
    return factor_of


def noise(key, extent, scale, limit, split=(), kind=jnp.bfloat16):
    values = scale * jax.random.normal(key, extent, jnp.float32)
    if split:
        values = values * level_of(key, extent, split, -0.22, 0.18)
    return jnp.clip(values, -limit, limit).astype(kind)


def setup_inputs(seed: int = 0) -> dict:
    splits = jax.random.split(jax.random.key(seed), 4)
    histories = noise(splits[0], (CASES, NT, P_SIZE), 1.0, 6.0, ((1, 32),), jnp.float32)
    point_weight = jnp.clip(jnp.exp(math.log(2.0) - 1.3862944 * jax.random.uniform(splits[1], (P_SIZE,), jnp.float32) ** level_of(splits[1], (P_SIZE,), ((0, 8),), -0.2, 0.2)), 0.5, 2.0)
    basis = noise(splits[2], (P_SIZE, H), P_SIZE ** -0.5, 0.09375, ((0, 8), (1, 4)), jnp.float32)
    return dict(histories=histories, point_weight=point_weight, basis=basis)


def make_table(times, total, bins):
    freqs = jnp.arange(1, bins + 1, dtype=jnp.int32)
    phase_int = times[:, None] * freqs[None, :] % total
    angle = 2.0 * jnp.pi / total * phase_int.astype(jnp.float32)
    window = 0.5 - 0.5 * jnp.cos(2.0 * jnp.pi / total * times.astype(jnp.float32))
    scale = (window / jnp.sqrt(jnp.float32(total)))[:, None]
    return jnp.concatenate([jnp.cos(angle) * scale, -jnp.sin(angle) * scale], axis=1)

def reference(histories, point_weight, basis):
    table = make_table(jnp.arange(NT, dtype=jnp.int32), NT, F)
    spectrum = jnp.einsum('stp,tk->skp', histories, table, precision=lax.Precision.HIGHEST)
    weighted = (spectrum * point_weight[None, None, :]).reshape(CASES * 2 * F, P_SIZE)
    coeffs = jnp.dot(weighted, basis, precision=lax.Precision.HIGHEST, preferred_element_type=jnp.float32)
    return coeffs.reshape(CASES, 2, F, H)
```

```python
import jax
import jax.numpy as jnp
from jax import lax
from jax.sharding import PartitionSpec as P

F = 256


def make_table(times, total, bins):
    freqs = jnp.arange(1, bins + 1, dtype=jnp.int32)
    phase_int = times[:, None] * freqs[None, :] % total
    angle = 2.0 * jnp.pi / total * phase_int.astype(jnp.float32)
    window = 0.5 - 0.5 * jnp.cos(2.0 * jnp.pi / total * times.astype(jnp.float32))
    scale = (window / jnp.sqrt(jnp.float32(total)))[:, None]
    return jnp.concatenate([jnp.cos(angle) * scale, -jnp.sin(angle) * scale], axis=1)


def local(histories, point_weight, basis):
    freq_count = lax.axis_size("freq")
    pts_count = lax.axis_size("pts")
    cases, time_local, all_points = histories.shape
    pts_local = all_points // pts_count
    series = lax.all_to_all(histories, "pts", split_axis=2, concat_axis=1, tiled=True)
    plane_time = time_local * pts_count
    times = lax.axis_index("freq") * plane_time + jnp.arange(plane_time, dtype=jnp.int32)
    table = make_table(times, plane_time * freq_count, F)
    spectrum = jnp.einsum("stp,tk->skp", series, table, precision=lax.Precision.HIGH)
    spectrum = spectrum.reshape(cases, 2, F, pts_local)
    spectrum = lax.psum_scatter(spectrum, "freq", scatter_dimension=2, tiled=True)
    bins_local = spectrum.shape[2]
    harmonics = basis.shape[1] * freq_count
    weighted = (spectrum * point_weight).reshape(cases * 2 * bins_local, pts_local)
    full = lax.all_gather(basis, "freq", axis=1, tiled=True)
    partial_value = jnp.dot(
        weighted, full, precision=lax.Precision.HIGH, preferred_element_type=jnp.float32
    )
    partial_value = partial_value.reshape(cases, 2, bins_local, harmonics)
    return lax.psum_scatter(partial_value, "pts", scatter_dimension=3, tiled=True)


def solution(mesh):
    return jax.shard_map(
        local,
        mesh=mesh,
        in_specs=(P(None, ("freq", "pts"), None), P("pts"), P("pts", "freq")),
        out_specs=P(None, None, "freq", "pts"),
        check_vma=False,
    )
```

```python
import functools

import jax
import jax.numpy as jnp
from jax import lax
from jax.experimental import pallas as pl
from jax.experimental.pallas import tpu as pltpu
from jax.sharding import PartitionSpec as P

F = 256
AHEAD = 4
LAG = 2
GROUP = 2
MESH = pl.DeviceIdType.MESH


def make_table(times, total, bins, blocks):
    freqs = jnp.arange(1, bins + 1, dtype=jnp.int32)
    phase_int = freqs[:, None] * times[None, :] % total
    angle = 2.0 * jnp.pi / total * phase_int.astype(jnp.float32)
    window = 0.5 - 0.5 * jnp.cos(2.0 * jnp.pi / total * times.astype(jnp.float32))
    scale = (window / jnp.sqrt(jnp.float32(total)))[None, :]
    cos = (jnp.cos(angle) * scale).reshape(blocks, 1, bins // blocks, -1)
    sin = (-jnp.sin(angle) * scale).reshape(blocks, 1, bins // blocks, -1)
    return jnp.concatenate([cos, sin], axis=1).reshape(2 * bins, -1)


def split(x):
    high = x.astype(jnp.bfloat16)
    return high, (x - high.astype(jnp.float32)).astype(jnp.bfloat16)


def dot3(a, b):
    ah, al = a
    bh, bl = b
    dot = functools.partial(jnp.dot, preferred_element_type=jnp.float32)
    return dot(ah, bh) + (dot(ah, bl) + dot(al, bh))


def kernel(
    nf, np_, hist, table, weight, basis, out,
    h2, bas, rs, spec, wf, th, tl_, wh, wl, cown, csend, pland, fland,
    h_send, h_recv, h_own, b_send_r, b_send_l, b_recv, b_own,
    r_send, r_recv, p_send, p_recv, f_send, f_recv,
):
    cases, time_local, _ = hist.shape
    points = h2.shape[2]
    rows = rs.shape[2]
    per = np_ // nf
    ho = bas.shape[2]
    chips = np_ // 2
    me = lax.axis_index("freq")
    p = lax.axis_index("pts")
    core = lax.rem(p, 2)
    chip = lax.div(p, 2)
    right, left = jnp.minimum(me + 1, nf - 1), jnp.maximum(me - 1, 0)
    has_r, has_l = me < nf - 1, me > 0

    barrier = pltpu.get_barrier_semaphore()
    for d in range(1, np_):
        pl.semaphore_signal(barrier, inc=1, device_id={"pts": lax.rem(p + d, np_)}, device_id_type=MESH)

    @pl.when(has_r)
    def _():
        pl.semaphore_signal(barrier, inc=1, device_id={"freq": right}, device_id_type=MESH)

    @pl.when(has_l)
    def _():
        pl.semaphore_signal(barrier, inc=1, device_id={"freq": left}, device_id_type=MESH)

    inner = jnp.logical_and(has_l, has_r)

    @pl.when(inner)
    def _():
        pl.semaphore_wait(barrier, np_ + 1)

    @pl.when(jnp.logical_not(inner))
    def _():
        pl.semaphore_wait(barrier, np_)

    def b_copy(q, src, to, sems):
        return pltpu.make_async_remote_copy(
            src_ref=src, dst_ref=bas.at[q], send_sem=sems.at[q], recv_sem=b_recv.at[q],
            device_id={"freq": to}, device_id_type=MESH,
        )

    for u in range(per):
        q = me * per + u
        src = basis.at[:, u * ho:(u + 1) * ho]

        @pl.when(has_r)
        def _():
            b_copy(q, src, right, b_send_r).start()

        @pl.when(has_l)
        def _():
            b_copy(q, src, left, b_send_l).start()

        pltpu.make_async_copy(src, bas.at[q], b_own.at[u]).start()

    def b_forward(hop, u):
        @pl.when(me - hop >= 0)
        def _():
            q = (me - hop) * per + u
            copy = b_copy(q, bas.at[q], right, b_send_r)
            copy.wait_recv()

            @pl.when(has_r)
            def _():
                copy.start()

        @pl.when(me + hop <= nf - 1)
        def _():
            q = (me + hop) * per + u
            copy = b_copy(q, bas.at[q], left, b_send_l)
            copy.wait_recv()

            @pl.when(has_l)
            def _():
                copy.start()

    def h_copy(s, q, slot):
        return pltpu.make_async_remote_copy(
            src_ref=hist.at[s, :, pl.ds(pl.multiple_of(q * points, 128), points)],
            dst_ref=h2.at[s, pl.ds(pl.multiple_of(slot * time_local, 8), time_local), :],
            send_sem=h_send.at[s, q], recv_sem=h_recv.at[s, slot],
            device_id={"pts": q}, device_id_type=MESH,
        )

    def h_local(s):
        return pltpu.make_async_copy(
            hist.at[s, :, pl.ds(pl.multiple_of(p * points, 128), points)],
            h2.at[s, pl.ds(pl.multiple_of(p * time_local, 8), time_local), :],
            h_own.at[s],
        )

    def h_start(s):
        for d in range(1, np_):
            h_copy(s, lax.rem(p + d, np_), p).start()
        h_local(s).start()

    for s in range(min(AHEAD, cases)):
        h_start(s)

    high, low = split(table[...])
    th[...] = high
    tl_[...] = low

    def r_copy(s, g, dst, to):
        return pltpu.make_async_remote_copy(
            src_ref=rs.at[s, g], dst_ref=rs.at[s, dst], send_sem=r_send.at[s, g], recv_sem=r_recv.at[s, dst],
            device_id={"freq": to}, device_id_type=MESH,
        )

    def own(g):
        return spec[pl.ds(pl.multiple_of(g * rows, 8), rows), :]

    hops = [(h, u) for h in range(1, nf - 1) for u in range(per)]
    steps = [1 + n * (cases - 1) // max(len(hops), 1) for n in range(len(hops))]

    def transform(i, carry):
        @pl.when(i + AHEAD < cases)
        def _():
            h_start(i + AHEAD)

        @pl.when(i < cases)
        def _():
            for d in range(1, np_):
                q = lax.rem(p + d, np_)
                h_copy(i, q, q).wait_recv()
            h_local(i).wait()
            spec[...] = dot3((th[...], tl_[...]), split(h2[i]))
            for d in range(nf - 1, 0, -1):
                @pl.when(me + d <= nf - 1)
                def _():
                    g = me + d
                    copy = r_copy(i, g, g, right)

                    @pl.when(has_l)
                    def _():
                        copy.wait_recv()
                        rs[i, g] = rs[i, g] + own(g)

                    @pl.when(jnp.logical_not(has_l))
                    def _():
                        rs[i, g] = own(g)

                    copy.start()

                @pl.when(me - d >= 0)
                def _():
                    g = me - d

                    @pl.when(has_r)
                    def _():
                        r_copy(i, g, g, left).wait_recv()
                        rs[i, g] = rs[i, g] + own(g)

                    @pl.when(jnp.logical_not(has_r))
                    def _():
                        rs[i, g] = own(g)

                    r_copy(i, g, nf if d == 1 else g, left).start()

            wf[lax.rem(i, LAG + 1)] = own(me)

        for (hop, u), step in zip(hops, steps):
            @pl.when(i == step)
            def _():
                b_forward(hop, u)

        @pl.when(i >= LAG)
        def _():
            j = i - LAG
            slot = lax.rem(j, LAG + 1)

            @pl.when(has_l)
            def _():
                r_copy(j, me, me, right).wait_recv()
                wf[slot] = wf[slot] + rs[j, me]

            @pl.when(has_r)
            def _():
                r_copy(j, nf, nf, left).wait_recv()
                wf[slot] = wf[slot] + rs[j, nf]

            high, low = split(wf[slot] * weight[...])
            at = pl.ds(pl.multiple_of(j * rows, 16), rows)
            wh[at, :] = high
            wl[at, :] = low

        return carry

    lax.fori_loop(0, cases + LAG, transform, 0)

    for u in range(per):
        b_forward(nf - 1, u)
        q = me * per + u
        pltpu.make_async_copy(basis.at[:, u * ho:(u + 1) * ho], bas.at[q], b_own.at[u]).wait()

    groups, tall = pland.shape[0], pland.shape[2]

    def p_copy(j, slot):
        return pltpu.make_async_remote_copy(
            src_ref=csend.at[slot], dst_ref=pland.at[j], send_sem=p_send.at[slot], recv_sem=p_recv.at[j],
            device_id={"pts": chip * 2 + 1 - core}, device_id_type=MESH,
        )

    def f_copy(j, c, slot):
        return pltpu.make_async_remote_copy(
            src_ref=pland.at[j, c], dst_ref=fland.at[j, slot], send_sem=f_send.at[j, c], recv_sem=f_recv.at[j, slot],
            device_id={"pts": c * 2 + core}, device_id_type=MESH,
        )

    def fit(i, carry):
        @pl.when(i < groups)
        def _():
            slot = lax.rem(i, 2)
            at = pl.ds(pl.multiple_of(i * tall, 16), tall)

            @pl.when(i >= 2)
            def _():
                p_copy(i - 2, slot).wait_send()

            def send_part(c, carry):
                csend[slot, c] = dot3((wh[at, :], wl[at, :]), split(bas[c * 2 + 1 - core]))
                return carry

            lax.fori_loop(0, chips, send_part, 0)
            p_copy(i, slot).start()

            def own_part(c, carry):
                cown[c] = dot3((wh[at, :], wl[at, :]), split(bas[c * 2 + core]))
                return carry

            lax.fori_loop(0, chips, own_part, 0)

        @pl.when(i < groups)
        def _():
            p_copy(i, lax.rem(i, 2)).wait_recv()
            pland[i, chip] = pland[i, chip] + cown[chip]
            for d in range(1, chips):
                c = lax.rem(chip + d, chips)
                pland[i, c] = pland[i, c] + cown[c]
                f_copy(i, c, chip).start()

        @pl.when(i >= 1)
        def _():
            j = i - 1
            total = pland[j, chip]
            for d in range(1, chips):
                c = lax.rem(chip + d, chips)
                f_copy(j, c, c).wait_recv()
                total = total + fland[j, c]
            out[pl.ds(pl.multiple_of(j * tall, 8), tall), :] = total

        return carry

    lax.fori_loop(0, groups + 1, fit, 0)

    def drain(s, carry):
        for d in range(1, np_):
            h_copy(s, lax.rem(p + d, np_), p).wait_send()
        for d in range(1, nf):
            @pl.when(me + d <= nf - 1)
            def _():
                r_copy(s, me + d, me + d, right).wait_send()

            @pl.when(me - d >= 0)
            def _():
                r_copy(s, me - d, me - d, left).wait_send()
        return carry

    lax.fori_loop(0, cases, drain, 0)
    for q in range(np_):
        @pl.when(jnp.logical_and(q // per <= me, has_r))
        def _():
            b_copy(q, bas.at[q], right, b_send_r).wait_send()

        @pl.when(jnp.logical_and(q // per >= me, has_l))
        def _():
            b_copy(q, bas.at[q], left, b_send_l).wait_send()

    for j in range(max(groups - 2, 0), groups):
        p_copy(j, j % 2).wait_send()
    for j in range(groups):
        for d in range(1, chips):
            f_copy(j, lax.rem(chip + d, chips), chip).wait_send()


def local(histories, point_weight, basis):
    nf = lax.axis_size("freq")
    np_ = lax.axis_size("pts")
    cases, time_local, all_points = histories.shape
    points = all_points // np_
    plane_time = time_local * np_
    rows = 2 * F // nf
    ho = basis.shape[1] * nf // np_
    chips = np_ // 2
    tall = GROUP * rows
    groups = cases // GROUP
    times = lax.axis_index("freq") * plane_time + jnp.arange(plane_time, dtype=jnp.int32)
    table = make_table(times, plane_time * nf, F, nf)
    f32, bf16 = jnp.float32, jnp.bfloat16
    hbm = pl.BlockSpec(memory_space=pl.ANY)
    vmem = pl.BlockSpec(memory_space=pltpu.VMEM)
    dma = pltpu.SemaphoreType.DMA
    coeffs = pl.pallas_call(
        functools.partial(kernel, nf, np_),
        out_shape=jax.ShapeDtypeStruct((cases * rows, ho), f32),
        in_specs=[hbm, vmem, vmem, hbm],
        out_specs=vmem,
        scratch_shapes=[
            pltpu.VMEM((cases, plane_time, points), f32),
            pltpu.VMEM((np_, points, ho), f32),
            pltpu.VMEM((cases, nf + 1, rows, points), f32),
            pltpu.VMEM((2 * F, points), f32),
            pltpu.VMEM((LAG + 1, rows, points), f32),
            pltpu.VMEM((2 * F, plane_time), bf16),
            pltpu.VMEM((2 * F, plane_time), bf16),
            pltpu.VMEM((cases * rows, points), bf16),
            pltpu.VMEM((cases * rows, points), bf16),
            pltpu.VMEM((chips, tall, ho), f32),
            pltpu.VMEM((2, chips, tall, ho), f32),
            pltpu.VMEM((groups, chips, tall, ho), f32),
            pltpu.VMEM((groups, chips, tall, ho), f32),
            dma((cases, np_)), dma((cases, np_)), dma((cases,)),
            dma((np_,)), dma((np_,)), dma((np_,)), dma((basis.shape[1] // ho,)),
            dma((cases, nf)), dma((cases, nf + 1)),
            dma((2,)), dma((groups,)),
            dma((groups, chips)), dma((groups, chips)),
        ],
        compiler_params=pltpu.CompilerParams(
            collective_id=0, has_side_effects=True, vmem_limit_bytes=60 * 1024 * 1024
        ),
    )(histories, table, point_weight.reshape(1, -1), basis)
    return coeffs.reshape(cases, 2, rows // 2, ho)


def solution(mesh):
    return jax.shard_map(
        local,
        mesh=mesh,
        in_specs=(P(None, ("freq", "pts"), None), P("pts"), P("pts", "freq")),
        out_specs=P(None, None, "freq", "pts"),
        check_vma=False,
    )
```

```python
import functools

import jax
import jax.numpy as jnp
from jax import lax
from jax.experimental import pallas as pl
from jax.experimental.pallas import tpu as pltpu
from jax.sharding import PartitionSpec as P

F = 256
AHEAD = 4
LAG = 2
CH = 2
FIRST = 4
OWN = 4
RATE = 0.5
HOP = 1.0
BASE = 0.0
GROUP = 2
MESH = pl.DeviceIdType.MESH


def make_table(times, total, bins, blocks):
    freqs = jnp.arange(1, bins + 1, dtype=jnp.int32)
    phase_int = freqs[:, None] * times[None, :] % total
    angle = 2.0 * jnp.pi / total * phase_int.astype(jnp.float32)
    window = 0.5 - 0.5 * jnp.cos(2.0 * jnp.pi / total * times.astype(jnp.float32))
    scale = (window / jnp.sqrt(jnp.float32(total)))[None, :]
    cos = (jnp.cos(angle) * scale).reshape(blocks, 1, bins // blocks, -1)
    sin = (-jnp.sin(angle) * scale).reshape(blocks, 1, bins // blocks, -1)
    return jnp.concatenate([cos, sin], axis=1).reshape(2 * bins, -1)


def split(x):
    high = x.astype(jnp.bfloat16)
    return high, (x - high.astype(jnp.float32)).astype(jnp.bfloat16)


def dot3(a, b):
    ah, al = a
    bh, bl = b
    dot = functools.partial(jnp.dot, preferred_element_type=jnp.float32)
    return dot(ah, bh) + (dot(ah, bl) + dot(al, bh))


def kernel(
    nf, np_, hist, table, weight, basis, out,
    h2, bas, rs, spec, wf, th, tl_, wh, wl, cown, csend, pland, fland,
    h_send, h_recv, h_own, b_send_r, b_send_l, b_recv, b_own,
    r_send, r_recv, p_send, p_recv, f_send, f_recv, o_sem,
):
    cases, time_local, _ = hist.shape
    points = h2.shape[2]
    rows = rs.shape[2]
    per = np_ // nf
    ho = bas.shape[2]
    chips = np_ // 2
    me = lax.axis_index("freq")
    p = lax.axis_index("pts")
    core = lax.rem(p, 2)
    chip = lax.div(p, 2)
    right, left = jnp.minimum(me + 1, nf - 1), jnp.maximum(me - 1, 0)
    has_r, has_l = me < nf - 1, me > 0

    barrier = pltpu.get_barrier_semaphore()
    for d in range(1, np_):
        pl.semaphore_signal(barrier, inc=1, device_id={"pts": lax.rem(p + d, np_)}, device_id_type=MESH)

    @pl.when(has_r)
    def _():
        pl.semaphore_signal(barrier, inc=1, device_id={"freq": right}, device_id_type=MESH)

    @pl.when(has_l)
    def _():
        pl.semaphore_signal(barrier, inc=1, device_id={"freq": left}, device_id_type=MESH)

    inner = jnp.logical_and(has_l, has_r)

    @pl.when(inner)
    def _():
        pl.semaphore_wait(barrier, np_ + 1)

    @pl.when(jnp.logical_not(inner))
    def _():
        pl.semaphore_wait(barrier, np_)

    part = points // CH
    chunks = per * CH

    def b_copy(g, n, to, sems, src=None):
        q = g * per + n // CH
        dst = bas.at[q, pl.ds(n % CH * part, part), :]
        return pltpu.make_async_remote_copy(
            src_ref=dst if src is None else src, dst_ref=dst,
            send_sem=sems.at[g, n], recv_sem=b_recv.at[g, n],
            device_id={"freq": to}, device_id_type=MESH,
        )

    def b_source(n):
        u = n // CH
        return basis.at[pl.ds(n % CH * part, part), u * ho:(u + 1) * ho]

    def b_local(n):
        return pltpu.make_async_copy(
            b_source(n), bas.at[me * per + n // CH, pl.ds(n % CH * part, part), :], b_own.at[n]
        )

    def b_start(n):
        @pl.when(has_r)
        def _():
            b_copy(me, n, right, b_send_r, b_source(n)).start()

        @pl.when(has_l)
        def _():
            b_copy(me, n, left, b_send_l, b_source(n)).start()

    def b_forward(hop, n):
        @pl.when(me - hop >= 0)
        def _():
            copy = b_copy(me - hop, n, right, b_send_r)
            copy.wait_recv()

            @pl.when(has_r)
            def _():
                copy.start()

        @pl.when(me + hop <= nf - 1)
        def _():
            copy = b_copy(me + hop, n, left, b_send_l)
            copy.wait_recv()

            @pl.when(has_l)
            def _():
                copy.start()

    first = FIRST
    plan = {}
    for n in range(chunks):
        if n >= OWN:
            plan.setdefault(int((n - OWN) * RATE), []).append((0, n))
        for hop in range(1, nf - 1):
            plan.setdefault(min(int(BASE + n * RATE + hop * HOP), first), []).append((hop, n))
    for n in range(chunks):
        if n < OWN:
            b_start(n)

    def h_copy(s, q, slot):
        return pltpu.make_async_remote_copy(
            src_ref=hist.at[s, :, pl.ds(pl.multiple_of(q * points, 128), points)],
            dst_ref=h2.at[s, pl.ds(pl.multiple_of(slot * time_local, 8), time_local), :],
            send_sem=h_send.at[s, q], recv_sem=h_recv.at[s, slot],
            device_id={"pts": q}, device_id_type=MESH,
        )

    def h_local(s):
        return pltpu.make_async_copy(
            hist.at[s, :, pl.ds(pl.multiple_of(p * points, 128), points)],
            h2.at[s, pl.ds(pl.multiple_of(p * time_local, 8), time_local), :],
            h_own.at[s],
        )

    def h_start(s):
        for d in range(1, np_):
            h_copy(s, lax.rem(p + d, np_), p).start()
        h_local(s).start()

    for s in range(min(AHEAD, cases)):
        h_start(s)

    high, low = split(table[...])
    th[...] = high
    tl_[...] = low

    def r_copy(s, g, dst, to):
        return pltpu.make_async_remote_copy(
            src_ref=rs.at[s, g], dst_ref=rs.at[s, dst], send_sem=r_send.at[s, g], recv_sem=r_recv.at[s, dst],
            device_id={"freq": to}, device_id_type=MESH,
        )

    def own(g):
        return spec[pl.ds(pl.multiple_of(g * rows, 8), rows), :]

    def transform(i):
        for step in sorted(plan):
            @pl.when(i == step)
            def _():
                for hop, n in plan[step]:
                    if hop:
                        b_forward(hop, n)
                    else:
                        b_start(n)

        @pl.when(i + AHEAD < cases)
        def _():
            h_start(i + AHEAD)

        @pl.when(i < cases)
        def _():
            for d in range(1, np_):
                q = lax.rem(p + d, np_)
                h_copy(i, q, q).wait_recv()
            h_local(i).wait()
            spec[...] = dot3((th[...], tl_[...]), split(h2[i]))
            for d in range(nf - 1, 0, -1):
                @pl.when(me + d <= nf - 1)
                def _():
                    g = me + d
                    copy = r_copy(i, g, g, right)

                    @pl.when(has_l)
                    def _():
                        copy.wait_recv()
                        rs[i, g] = rs[i, g] + own(g)

                    @pl.when(jnp.logical_not(has_l))
                    def _():
                        rs[i, g] = own(g)

                    copy.start()

                @pl.when(me - d >= 0)
                def _():
                    g = me - d

                    @pl.when(has_r)
                    def _():
                        r_copy(i, g, g, left).wait_recv()
                        rs[i, g] = rs[i, g] + own(g)

                    @pl.when(jnp.logical_not(has_r))
                    def _():
                        rs[i, g] = own(g)

                    r_copy(i, g, nf if d == 1 else g, left).start()

            wf[lax.rem(i, LAG + 1)] = own(me)

        @pl.when(jnp.logical_and(i >= LAG, i < cases + LAG))
        def _():
            j = i - LAG
            slot = lax.rem(j, LAG + 1)

            @pl.when(has_l)
            def _():
                r_copy(j, me, me, right).wait_recv()
                wf[slot] = wf[slot] + rs[j, me]

            @pl.when(has_r)
            def _():
                r_copy(j, nf, nf, left).wait_recv()
                wf[slot] = wf[slot] + rs[j, nf]

            high, low = split(wf[slot] * weight[...])
            at = pl.ds(pl.multiple_of(j * rows, 16), rows)
            wh[at, :] = high
            wl[at, :] = low

    groups, tall = pland.shape[0], pland.shape[2]

    def p_copy(j, c):
        return pltpu.make_async_remote_copy(
            src_ref=csend.at[j % 2, c], dst_ref=pland.at[j, c],
            send_sem=p_send.at[j % 2, c], recv_sem=p_recv.at[j, c],
            device_id={"pts": chip * 2 + 1 - core}, device_id_type=MESH,
        )

    def f_copy(j, c, slot):
        return pltpu.make_async_remote_copy(
            src_ref=pland.at[j, c], dst_ref=fland.at[j, slot], send_sem=f_send.at[j, c], recv_sem=f_recv.at[j, slot],
            device_id={"pts": c * 2 + core}, device_id_type=MESH,
        )

    def o_copy(j):
        return pltpu.make_async_copy(
            pland.at[j, chip], out.at[pl.ds(pl.multiple_of(j * tall, 8), tall), :], o_sem.at[j]
        )

    def fit(j):
        at = pl.ds(j * tall, tall)

        def pass_on(d):
            c = lax.rem(chip + d, chips)
            p_copy(j, c).wait_recv()
            pland[j, c] = pland[j, c] + cown[c]

            @pl.when(d < chips)
            def _():
                f_copy(j, c, chip).start()

        def part(d, carry):
            c = lax.rem(chip + d, chips)
            if j >= 2:
                p_copy(j - 2, c).wait_send()
            csend[j % 2, c] = dot3((wh[at, :], wl[at, :]), split(bas[c * 2 + 1 - core]))
            p_copy(j, c).start()
            cown[c] = dot3((wh[at, :], wl[at, :]), split(bas[c * 2 + core]))

            @pl.when(d > 1)
            def _():
                pass_on(d - 1)

            return carry

        lax.fori_loop(1, chips + 1, part, 0)
        pass_on(chips)

    def finish(j):
        total = pland[j, chip]
        for d in range(1, chips):
            c = lax.rem(chip + d, chips)
            f_copy(j, c, c).wait_recv()
            total = total + fland[j, c]
        pland[j, chip] = total
        o_copy(j).start()

    fits = [max(first + g, GROUP * (g + 1) - 1 + LAG) for g in range(groups)]

    def step(i, carry):
        transform(i)

        @pl.when(i == first)
        def _():
            for n in range(chunks):
                b_forward(nf - 1, n)
                b_local(n).wait()

        for g in range(groups):
            @pl.when(i == fits[g])
            def _():
                fit(g)

        return carry

    for n in range(chunks):
        b_local(n).start()
    lax.fori_loop(0, max(cases + LAG, fits[-1] + 1), step, 0)
    for g in range(groups):
        finish(g)

    def drain(s, carry):
        for d in range(1, np_):
            h_copy(s, lax.rem(p + d, np_), p).wait_send()
        for d in range(1, nf):
            @pl.when(me + d <= nf - 1)
            def _():
                r_copy(s, me + d, me + d, right).wait_send()

            @pl.when(me - d >= 0)
            def _():
                r_copy(s, me - d, me - d, left).wait_send()
        return carry

    lax.fori_loop(0, cases, drain, 0)
    for g in range(nf):
        @pl.when(jnp.logical_and(g <= me, has_r))
        def _():
            for n in range(chunks):
                b_copy(g, n, right, b_send_r).wait_send()

        @pl.when(jnp.logical_and(g >= me, has_l))
        def _():
            for n in range(chunks):
                b_copy(g, n, left, b_send_l).wait_send()

    for j in range(groups):
        o_copy(j).wait()
    for j in range(max(groups - 2, 0), groups):
        for c in range(chips):
            p_copy(j, c).wait_send()
    for j in range(groups):
        for d in range(1, chips):
            f_copy(j, lax.rem(chip + d, chips), chip).wait_send()


def local(histories, point_weight, basis):
    nf = lax.axis_size("freq")
    np_ = lax.axis_size("pts")
    cases, time_local, all_points = histories.shape
    points = all_points // np_
    plane_time = time_local * np_
    rows = 2 * F // nf
    ho = basis.shape[1] * nf // np_
    chunks = np_ // nf * CH
    chips = np_ // 2
    tall = GROUP * rows
    groups = cases // GROUP
    times = lax.axis_index("freq") * plane_time + jnp.arange(plane_time, dtype=jnp.int32)
    table = make_table(times, plane_time * nf, F, nf)
    f32, bf16 = jnp.float32, jnp.bfloat16
    hbm = pl.BlockSpec(memory_space=pl.ANY)
    vmem = pl.BlockSpec(memory_space=pltpu.VMEM)
    dma = pltpu.SemaphoreType.DMA
    coeffs = pl.pallas_call(
        functools.partial(kernel, nf, np_),
        out_shape=jax.ShapeDtypeStruct((cases * rows, ho), f32),
        in_specs=[hbm, vmem, vmem, hbm],
        out_specs=hbm,
        scratch_shapes=[
            pltpu.VMEM((cases, plane_time, points), f32),
            pltpu.VMEM((np_, points, ho), f32),
            pltpu.VMEM((cases, nf + 1, rows, points), f32),
            pltpu.VMEM((2 * F, points), f32),
            pltpu.VMEM((LAG + 1, rows, points), f32),
            pltpu.VMEM((2 * F, plane_time), bf16),
            pltpu.VMEM((2 * F, plane_time), bf16),
            pltpu.VMEM((cases * rows, points), bf16),
            pltpu.VMEM((cases * rows, points), bf16),
            pltpu.VMEM((chips, tall, ho), f32),
            pltpu.VMEM((2, chips, tall, ho), f32),
            pltpu.VMEM((groups, chips, tall, ho), f32),
            pltpu.VMEM((groups, chips, tall, ho), f32),
            dma((cases, np_)), dma((cases, np_)), dma((cases,)),
            dma((nf, chunks)), dma((nf, chunks)), dma((nf, chunks)), dma((chunks,)),
            dma((cases, nf)), dma((cases, nf + 1)),
            dma((2, chips)), dma((groups, chips)),
            dma((groups, chips)), dma((groups, chips)), dma((groups,)),
        ],
        compiler_params=pltpu.CompilerParams(
            collective_id=0, has_side_effects=True, vmem_limit_bytes=60 * 1024 * 1024
        ),
    )(histories, table, point_weight.reshape(1, -1), basis)
    return coeffs.reshape(cases, 2, rows // 2, ho)


def solution(mesh):
    return jax.shard_map(
        local,
        mesh=mesh,
        in_specs=(P(None, ("freq", "pts"), None), P("pts"), P("pts", "freq")),
        out_specs=P(None, None, "freq", "pts"),
        check_vma=False,
    )
```
